32 devices in a mesh: groups: 2 (over y), seq: 16 (over z, x, core).
Axes of the slice: x: 2, y: 2, z: 4, core: 2. Of those that a mesh axis runs over, the one named last changes fastest.
Arguments:
- token_ids: int32 [4096], P('groups'), parts along dimension 0, may hold values from 0 to 511
- vocab_table: bfloat16 [512, 3, 4096], P(None, None, 'seq'), may hold values from -6 to 6
- short_filter: float32 [7, 3, 4096], replicated, may hold values from -2 to 2
- residue: float32 [4096, 16], replicated, may hold values from -1.5 to 1.5
- decay: float32 [4096, 16], replicated, may hold values from 0.2 to 64
- skip_gain: float32 [4096], replicated, may hold values from -3 to 3
Outputs:
- hyena_out: bfloat16 [4096, 4096], P(('groups', 'seq')), parts along dimension 0
The draws below stay inside these ranges and needn't reach their ends.
There are 2 independent parts, one for each index of `groups`. The reference program is written for one: setup_inputs(seed, part) draws one part's arguments, and reference() takes and returns one part's arrays. A program takes and returns all parts, laid end to end along the dimension named above; an argument that names none is the same for every part. Nothing has to cross between parts.
All inputs are finite; a program needn't handle non-finite values.
Results may differ from the reference program's by a relative error of at most 0.012.
Values may be sent and summed in bfloat16 or wider, within the bound.
A program may use at most 192 MiB of HBM per device.

```python
import math
import jax
import jax.numpy as jnp
from jax import lax

D = 4096
VOCAB = 512
SHORT = 7
POLES = 16
SEQ_LEN = 2048


def plant(entries, stream_key, least, top_value):
    spot = [jax.random.randint(jax.random.fold_in(stream_key, axis), (), 0, length) for axis, length in enumerate(entries.shape)]
    main_axis = entries.shape.index(max(entries.shape))
    neighbour = spot[:main_axis] + [(spot[main_axis] + 1) % entries.shape[main_axis]] + spot[main_axis + 1:]
    return entries.at[tuple(spot)].set(least).at[tuple(neighbour)].set(top_value)


def shard_levels(own_key, extent, split, least, high):
    loudness, own = 1.0, jax.random.fold_in(own_key, 6)
    for dim, blocks in split:
        steps = jnp.exp(jax.random.uniform(jax.random.fold_in(own, dim), (blocks,), jnp.float32, least / len(split), high / len(split)))
        loudness = loudness * jnp.repeat(steps, extent[dim] // blocks).reshape([-1 if axis == dim else 1 for axis in range(len(extent))])
    return loudness


def gaussian(stream_key, dims, scale, limit, cuts=(), kind=jnp.bfloat16):
    array = jax.random.normal(stream_key, dims, jnp.float32) * scale
    if len(cuts) > 0:
        array = shard_levels(stream_key, dims, cuts, -0.22, 0.18) * array
    return jnp.clip(array, min=-limit, max=limit).astype(kind)


def setup_inputs(seed: int = 0, part: int = 0) -> dict:
    splits = jax.random.split(jax.random.key(seed), 7)
    part_keys = jax.random.split(jax.random.fold_in(splits[6], part), 7)
    token_ids = plant(jax.random.randint(part_keys[0], (SEQ_LEN,), 0, VOCAB), jax.random.fold_in(part_keys[0], 1), 0, VOCAB - 1).astype(jnp.int32)
    vocab_table = gaussian(splits[1], (VOCAB, 3, D), 1.0, 6.0, ((2, 16),))
    short_filter = gaussian(splits[2], (SHORT, 3, D), SHORT ** -0.5, 2.0, (), jnp.float32)
    residue = gaussian(splits[3], (D, POLES), 0.25, 1.5, (), jnp.float32)
    decay = jnp.clip(jnp.exp(jax.random.uniform(splits[4], (D, POLES), jnp.float32, math.log(0.2), math.log(64.0))), 0.2, 64.0)
    skip_gain = gaussian(splits[5], (D,), 0.5, 3.0, (), jnp.float32)
    return {"token_ids": token_ids, "vocab_table": vocab_table, "short_filter": short_filter, "residue": residue, "decay": decay, "skip_gain": skip_gain}


def filter_spectrum(freq, total, pole, gap, tail, scale):
    theta = freq.astype(jnp.float32) * (2.0 * math.pi / total)
    sine = jnp.sin(theta)[:, None]
    halfsq = (jnp.sin(0.5 * theta) ** 2)[:, None]
    parity = (1 - 2 * (freq % 2)).astype(jnp.float32)[:, None]
    real_part = jnp.zeros((freq.shape[0], pole.shape[0]), jnp.float32)
    imag_part = jnp.zeros((freq.shape[0], pole.shape[0]), jnp.float32)
    for mode in range(pole.shape[1]):
        dreal = gap[:, mode] + 2.0 * pole[:, mode] * halfsq
        dimag = pole[:, mode] * sine
        factor = scale[:, mode] * (1.0 - tail[:, mode] * parity) / (dreal * dreal + dimag * dimag)
        real_part = real_part + factor * dreal
        imag_part = imag_part - factor * dimag
    return (real_part, imag_part)

def reference(token_ids, vocab_table, short_filter, residue, decay, skip_gain):
    length = token_ids.shape[0]
    total = 2 * length
    streams = jnp.take(vocab_table, token_ids, axis=0).astype(jnp.float32)
    rim = short_filter.shape[0] - 1
    padded = jnp.pad(streams, ((rim, 0), (0, 0), (0, 0)))
    mixed = jnp.zeros(streams.shape, jnp.float32)
    for lag in range(rim + 1):
        mixed = mixed + short_filter[lag] * padded[rim - lag:rim - lag + length]
    query = mixed[:, 0]
    gated = mixed[:, 1] * mixed[:, 2]
    rate = decay / length
    pole = jnp.exp(-rate)
    gap = -jnp.expm1(-rate)
    tail = jnp.exp(-decay)
    scale = residue * jnp.sqrt(2.0 * rate)
    width = gated.shape[1]
    group = min(width, 256)
    count = width // group
    modes = pole.shape[1]

    def one_block(items):
        block_gated, block_pole, block_gap, block_tail, block_scale = items
        spectrum_gated = jnp.fft.rfft(block_gated, n=total, axis=0)
        freq = jnp.arange(length + 1, dtype=jnp.int32)
        filt_real, filt_imag = filter_spectrum(freq, total, block_pole, block_gap, block_tail, block_scale)
        product = spectrum_gated * lax.complex(filt_real, filt_imag)
        return jnp.fft.irfft(product, n=total, axis=0)[:length]
    blocks = gated.reshape(length, count, group).transpose(1, 0, 2)
    convolved = lax.map(one_block, (blocks, pole.reshape(count, group, modes), gap.reshape(count, group, modes), tail.reshape(count, group, modes), scale.reshape(count, group, modes)))
    convolved = convolved.transpose(1, 0, 2).reshape(length, width)
    result = convolved + skip_gain * gated
    return (query * result).astype(jnp.bfloat16)
```

```python
import functools
import math

import jax
import jax.numpy as jnp
from jax import lax
from jax.experimental import pallas as pl
from jax.experimental.pallas import tpu as pltpu
from jax.sharding import PartitionSpec as P

HIGHEST = lax.Precision.HIGHEST


def angle_tables(first_index, second_index, modulus):
    product = first_index[:, None] * second_index[None, :] % modulus
    angle = product.astype(jnp.float32) * (2.0 * math.pi / modulus)
    return (jnp.cos(angle), jnp.sin(angle))


def short_conv(padded, taps, count):
    width = taps.shape[0]
    total = jnp.zeros((count,) + padded.shape[1:], jnp.float32)
    for lag in range(width):
        start = width - 1 - lag
        total = total + taps[lag] * padded[start : start + count].astype(jnp.float32)
    return total


def filter_spectrum(freq, total, pole, gap, tail, scale):
    theta = freq.astype(jnp.float32) * (2.0 * math.pi / total)
    sine = jnp.sin(theta)[:, :, None, None]
    halfsq = (jnp.sin(0.5 * theta) ** 2)[:, :, None, None]
    parity = (1 - 2 * (freq % 2)).astype(jnp.float32)[:, :, None, None]
    shape_out = freq.shape + (pole.shape[0],)
    real_part = jnp.zeros(shape_out, jnp.float32)
    imag_part = jnp.zeros(shape_out, jnp.float32)
    for first in range(0, pole.shape[1], 4):
        part_pole = pole[:, first : first + 4]
        dreal = gap[:, first : first + 4] + 2.0 * part_pole * halfsq
        dimag = part_pole * sine
        factor = (
            scale[:, first : first + 4]
            * (1.0 - tail[:, first : first + 4] * parity)
            / (dreal * dreal + dimag * dimag)
        )
        real_part = real_part + jnp.sum(factor * dreal, axis=-1)
        imag_part = imag_part - jnp.sum(factor * dimag, axis=-1)
    return (real_part, imag_part)


def convolve(gated, skip, filters, total, move_forward, move_back):
    pieces, block, width = gated.shape
    span = 2 * pieces
    outer_index = jnp.arange(span, dtype=jnp.int32)
    piece_index = jnp.arange(pieces, dtype=jnp.int32)
    outer_cos, outer_sin = angle_tables(outer_index, piece_index, span)
    real_part = jnp.einsum("kp,ptc->ktc", outer_cos, gated, precision=HIGHEST)
    imag_part = -jnp.einsum("kp,ptc->ktc", outer_sin, gated, precision=HIGHEST)
    times = jnp.arange(block, dtype=jnp.int32)
    twist_cos, twist_sin = angle_tables(outer_index, times, total)
    twist_cos = twist_cos[:, :, None]
    twist_sin = twist_sin[:, :, None]
    turned_real = twist_cos * real_part + twist_sin * imag_part
    turned_imag = twist_cos * imag_part - twist_sin * real_part
    moved = move_forward(jnp.stack([turned_real, turned_imag]))
    count = moved.shape[1]
    length = moved.shape[2]
    positions = jnp.arange(length, dtype=jnp.int32)
    inner_cos, inner_sin = angle_tables(positions, positions, length)
    freq_real = jnp.einsum("mt,ktc->kmc", inner_cos, moved[0], precision=HIGHEST) + jnp.einsum(
        "mt,ktc->kmc", inner_sin, moved[1], precision=HIGHEST
    )
    freq_imag = jnp.einsum("mt,ktc->kmc", inner_cos, moved[1], precision=HIGHEST) - jnp.einsum(
        "mt,ktc->kmc", inner_sin, moved[0], precision=HIGHEST
    )
    owned = jnp.arange(count, dtype=jnp.int32)
    freq = (owned[:, None] + span * positions[None, :]) % total
    filt_real, filt_imag = filter_spectrum(freq, total, *filters)
    prod_real = freq_real * filt_real - freq_imag * filt_imag
    prod_imag = freq_real * filt_imag + freq_imag * filt_real
    back_real = jnp.einsum("mt,kmc->ktc", inner_cos, prod_real, precision=HIGHEST) - jnp.einsum(
        "mt,kmc->ktc", inner_sin, prod_imag, precision=HIGHEST
    )
    back_imag = jnp.einsum("mt,kmc->ktc", inner_cos, prod_imag, precision=HIGHEST) + jnp.einsum(
        "mt,kmc->ktc", inner_sin, prod_real, precision=HIGHEST
    )
    undo_cos, undo_sin = angle_tables(owned, positions, total)
    undo_cos = undo_cos[:, :, None]
    undo_sin = undo_sin[:, :, None]
    untwist_real = undo_cos * back_real - undo_sin * back_imag
    untwist_imag = undo_cos * back_imag + undo_sin * back_real
    returned = move_back(jnp.stack([untwist_real, untwist_imag]))
    last_cos, last_sin = angle_tables(piece_index, outer_index, span)
    convolved = (
        jnp.einsum("pk,ktc->ptc", last_cos, returned[0], precision=HIGHEST)
        - jnp.einsum("pk,ktc->ptc", last_sin, returned[1], precision=HIGHEST)
    ) * (1.0 / total)
    return convolved + skip * gated


def unchanged(value):
    return value


def body(token_ids, vocab_table, short_filter, residue, decay, skip_gain):
    pieces = lax.axis_size("seq")
    place = lax.axis_index("seq")
    length = token_ids.shape[0]
    local = length // pieces
    share = vocab_table.shape[2]
    rim = short_filter.shape[0] - 1
    total = 2 * length
    rate = decay / length
    pole = jnp.exp(-rate)
    gap = -jnp.expm1(-rate)
    tail = jnp.exp(-decay)
    scale = residue * jnp.sqrt(2.0 * rate)
    first_channel = place * share
    chan_taps = lax.dynamic_slice_in_dim(short_filter, first_channel, share, 2)
    chan_filters = (
        lax.dynamic_slice_in_dim(pole, first_channel, share, 0),
        lax.dynamic_slice_in_dim(gap, first_channel, share, 0),
        lax.dynamic_slice_in_dim(tail, first_channel, share, 0),
        lax.dynamic_slice_in_dim(scale, first_channel, share, 0),
    )
    chan_skip = lax.dynamic_slice_in_dim(skip_gain, first_channel, share, 0)
    streams = jnp.take(vocab_table, token_ids, axis=0)
    padded = jnp.pad(streams, ((rim, 0), (0, 0), (0, 0)))
    mixed = short_conv(padded, chan_taps, length)
    query = mixed[:, 0]
    gated = (mixed[:, 1] * mixed[:, 2]).reshape(pieces, local, share)
    convolved = convolve(gated, chan_skip, chan_filters, total, unchanged, unchanged)
    output = (query * convolved.reshape(length, share)).astype(jnp.bfloat16)
    return lax.all_to_all(output, "seq", split_axis=0, concat_axis=1, tiled=True)


LANES = 128
SUB = 8
HALO = 8
UNROLL = 8
MESH = pl.DeviceIdType.MESH


def wide(row):
    return jnp.broadcast_to(row, (SUB, LANES))


def scan_kernel(
    pieces,
    local,
    width,
    modes,
    ids_ref,
    tab_ref,
    taps_ref,
    decay_ref,
    residue_ref,
    skip_ref,
    out_ref,
    hot_ref,
    x_ref,
    query_ref,
    gated_ref,
    end_ref,
    begin_ref,
    coef_ref,
    turn_ref,
    send_ref,
    send_sem,
    recv_sem,
    own_sem,
):
    me = lax.axis_index("seq")
    half = pieces // 2
    near = me // half
    slots = pieces // SUB
    parts = half // SUB
    share = skip_ref.shape[1]
    vocab = tab_ref.shape[0]
    blocks = share // LANES
    length = pieces * local
    barrier = pltpu.get_barrier_semaphore()
    for step in range(1, pieces):
        peer = lax.rem(me + step, pieces)
        pl.semaphore_signal(barrier, inc=1, device_id={"seq": peer}, device_id_type=MESH)

    rows = (HALO + local) * pieces
    cut = rows // 4
    for i in range(4):
        span = pl.ds(i * cut, cut)
        entry = lax.broadcasted_iota(jnp.int32, (cut, vocab), 1)
        hot_ref[span, :] = jnp.where(ids_ref[span, :] == entry, 1.0, 0.0).astype(jnp.bfloat16)

    def remote(block, peer, source):
        column = pl.ds(pl.multiple_of(source * share + block * LANES, LANES), LANES)
        return pltpu.make_async_remote_copy(
            src_ref=send_ref.at[block, peer],
            dst_ref=out_ref.at[:, column],
            send_sem=send_sem.at[block, peer],
            recv_sem=recv_sem.at[block, source],
            device_id={"seq": peer},
            device_id_type=MESH,
        )

    def own(block):
        column = pl.ds(pl.multiple_of(me * share + block * LANES, LANES), LANES)
        return pltpu.make_async_copy(send_ref.at[block, me], out_ref.at[:, column], own_sem.at[block])

    for block in range(blocks):
        lane = pl.ds(block * LANES, LANES)
        rate = decay_ref[:, lane] / length
        pole = jnp.exp(-rate)
        leap = jnp.exp(-rate * local)
        coef_ref[0] = pole
        coef_ref[1] = residue_ref[:, lane] * jnp.sqrt(2.0 * rate)
        skip = wide(skip_ref[:, lane])
        table = tab_ref[:, block * 3 * LANES : (block + 1) * 3 * LANES]
        for i in range(4):
            span = pl.ds(i * cut, cut)
            x_ref[span, :] = jnp.dot(hot_ref[span, :], table, preferred_element_type=jnp.float32)

        def first_pass(slot, _):
            base = pl.multiple_of(slot * SUB, SUB)
            poles = [wide(coef_ref[0, s : s + 1, :]) for s in range(modes)]
            taps = [
                [wide(taps_ref[lag, j : j + 1, lane]) for lag in range(width)] for j in range(3)
            ]

            def step(i, state):
                state = list(state)
                mixed = []
                for j in range(3):
                    seen = {}
                    for t in range(1 - width, UNROLL):
                        at = pl.multiple_of((i * UNROLL + t + HALO) * pieces + base, SUB)
                        seen[t] = x_ref[pl.ds(at, SUB), j * LANES : (j + 1) * LANES]
                    totals = []
                    for t in range(UNROLL):
                        total = taps[j][0] * seen[t]
                        for lag in range(1, width):
                            total = total + taps[j][lag] * seen[t - lag]
                        totals.append(total)
                    mixed.append(totals)
                for t in range(UNROLL):
                    at = pl.multiple_of((i * UNROLL + t) * pieces + base, SUB)
                    gated = mixed[1][t] * mixed[2][t]
                    query_ref[pl.ds(at, SUB), :] = mixed[0][t]
                    gated_ref[pl.ds(at, SUB), :] = gated
                    for s in range(modes):
                        state[s] = poles[s] * state[s] + gated
                return tuple(state)

            zero = jnp.zeros((SUB, LANES), jnp.float32)
            state = lax.fori_loop(0, local // UNROLL, step, (zero,) * modes)
            for s in range(modes):
                end_ref[pl.ds(pl.multiple_of(s * pieces + base, SUB), SUB), :] = state[s]
            return 0

        lax.fori_loop(0, slots, first_pass, 0)
        carry = jnp.zeros((modes, LANES), jnp.float32)
        for k in range(pieces):
            begin_ref[pl.ds(k, modes, stride=pieces), :] = carry
            carry = leap * carry + end_ref[pl.ds(k, modes, stride=pieces), :]

        for side in range(2):
            group = near if side else 1 - near
            for part in range(parts):
                first = group * half + part * SUB
                base = pl.multiple_of(first, SUB)
                poles = [wide(coef_ref[0, s : s + 1, :]) for s in range(modes)]
                coefs = [wide(coef_ref[1, s : s + 1, :]) for s in range(modes)]

                def step(i, state):
                    state = list(state)
                    for t in range(UNROLL):
                        at = pl.multiple_of((i * UNROLL + t) * pieces + base, SUB)
                        gated = gated_ref[pl.ds(at, SUB), :]
                        terms = [skip * gated]
                        for s in range(modes):
                            state[s] = poles[s] * state[s] + gated
                            terms.append(coefs[s] * state[s])
                            if len(terms) == 5:
                                terms = [((terms[0] + terms[1]) + (terms[2] + terms[3])) + terms[4]]
                        total = terms[0]
                        for term in terms[1:]:
                            total = total + term
                        turn_ref[pl.ds(pl.multiple_of((i * UNROLL + t) * SUB, SUB), SUB), :] = (
                            query_ref[pl.ds(at, SUB), :] * total
                        )
                    return tuple(state)

                state = tuple(
                    begin_ref[pl.ds(pl.multiple_of(s * pieces + base, SUB), SUB), :]
                    for s in range(modes)
                )
                lax.fori_loop(0, local // UNROLL, step, state)
                for k in range(SUB):
                    send_ref[block, first + k] = turn_ref[pl.ds(k, local, stride=SUB), :].astype(
                        jnp.bfloat16
                    )
                if block == 0 and side == 0 and part == 0:
                    pl.semaphore_wait(barrier, pieces - 1)
                for k in range(SUB):
                    peer = first + lax.rem(me + k, SUB)
                    if side == 0:
                        remote(block, peer, me).start()
                    else:

                        @pl.when(peer != me)
                        def _():
                            remote(block, peer, me).start()

                        @pl.when(peer == me)
                        def _():
                            own(block).start()

    for block in range(blocks):
        own(block).wait()
        for step in range(1, pieces):
            remote(block, lax.rem(me + step, pieces), me).wait_send()
        for step in range(1, pieces):
            remote(block, me, lax.rem(me + step, pieces)).wait_recv()


def scan_body(token_ids, vocab_table, short_filter, residue, decay, skip_gain):
    pieces = lax.axis_size("seq")
    place = lax.axis_index("seq")
    length = token_ids.shape[0]
    local = length // pieces
    vocab, streams, share = vocab_table.shape
    width = short_filter.shape[0]
    modes = decay.shape[1]
    blocks = share // LANES
    spread = jnp.concatenate(
        [
            jnp.concatenate([jnp.full((1, HALO), -1, jnp.int32), token_ids.reshape(pieces, local)[:-1, local - HALO :]]),
            token_ids.reshape(pieces, local),
        ],
        axis=1,
    )
    ids = spread.T.reshape((HALO + local) * pieces, 1)
    table = vocab_table.reshape(vocab, streams, blocks, LANES).transpose(0, 2, 1, 3)
    table = table.reshape(vocab, streams * share)
    start = place * share
    taps = lax.dynamic_slice_in_dim(short_filter, start, share, 2)
    chan_decay = lax.dynamic_slice_in_dim(decay, start, share, 0).T
    chan_residue = lax.dynamic_slice_in_dim(residue, start, share, 0).T
    skip = lax.dynamic_slice_in_dim(skip_gain, start, share, 0)[None]
    rows = (HALO + local) * pieces
    vmem = pl.BlockSpec(memory_space=pltpu.VMEM)
    return pl.pallas_call(
        functools.partial(scan_kernel, pieces, local, width, modes),
        out_shape=jax.ShapeDtypeStruct((local, pieces * share), jnp.bfloat16),
        in_specs=[vmem] * 6,
        out_specs=pl.BlockSpec(memory_space=pl.ANY),
        scratch_shapes=[
            pltpu.VMEM((rows, vocab), jnp.bfloat16),
            pltpu.VMEM((rows, streams * LANES), jnp.float32),
            pltpu.VMEM((length, LANES), jnp.float32),
            pltpu.VMEM((length, LANES), jnp.float32),
            pltpu.VMEM((modes * pieces, LANES), jnp.float32),
            pltpu.VMEM((modes * pieces, LANES), jnp.float32),
            pltpu.VMEM((2, modes, LANES), jnp.float32),
            pltpu.VMEM((local * SUB, LANES), jnp.float32),
            pltpu.VMEM((blocks, pieces, local, LANES), jnp.bfloat16),
            pltpu.SemaphoreType.DMA((blocks, pieces)),
            pltpu.SemaphoreType.DMA((blocks, pieces)),
            pltpu.SemaphoreType.DMA((blocks,)),
        ],
        compiler_params=pltpu.CompilerParams(collective_id=0, has_side_effects=True),
    )(ids, table, taps, chan_decay, chan_residue, skip)


def fits(mesh, share, local, width):
    pieces = mesh.shape["seq"]
    return share % LANES == 0 and pieces % (2 * SUB) == 0 and local % 16 == 0 and width <= HALO + 1


def solution(mesh):
    placed = (P("groups"), P(None, None, "seq"), P(), P(), P(), P())

    def whole(token_ids, vocab_table, short_filter, residue, decay, skip_gain):
        pieces = mesh.shape["seq"]
        local = token_ids.shape[0] // (mesh.shape["groups"] * pieces)
        share = vocab_table.shape[2] // pieces
        chosen = scan_body if fits(mesh, share, local, short_filter.shape[0]) else body
        return jax.shard_map(
            chosen, mesh=mesh, in_specs=placed, out_specs=P(("groups", "seq"), None), check_vma=False
        )(token_ids, vocab_table, short_filter, residue, decay, skip_gain)

    return whole
```

```python
import functools
import math

import jax
import jax.numpy as jnp
from jax import lax
from jax.experimental import pallas as pl
from jax.experimental.pallas import tpu as pltpu
from jax.sharding import PartitionSpec as P

HIGHEST = lax.Precision.HIGHEST


def angle_tables(first_index, second_index, modulus):
    product = first_index[:, None] * second_index[None, :] % modulus
    angle = product.astype(jnp.float32) * (2.0 * math.pi / modulus)
    return (jnp.cos(angle), jnp.sin(angle))


def short_conv(padded, taps, count):
    width = taps.shape[0]
    total = jnp.zeros((count,) + padded.shape[1:], jnp.float32)
    for lag in range(width):
        start = width - 1 - lag
        total = total + taps[lag] * padded[start : start + count].astype(jnp.float32)
    return total


def filter_spectrum(freq, total, pole, gap, tail, scale):
    theta = freq.astype(jnp.float32) * (2.0 * math.pi / total)
    sine = jnp.sin(theta)[:, :, None, None]
    halfsq = (jnp.sin(0.5 * theta) ** 2)[:, :, None, None]
    parity = (1 - 2 * (freq % 2)).astype(jnp.float32)[:, :, None, None]
    shape_out = freq.shape + (pole.shape[0],)
    real_part = jnp.zeros(shape_out, jnp.float32)
    imag_part = jnp.zeros(shape_out, jnp.float32)
    for first in range(0, pole.shape[1], 4):
        part_pole = pole[:, first : first + 4]
        dreal = gap[:, first : first + 4] + 2.0 * part_pole * halfsq
        dimag = part_pole * sine
        factor = (
            scale[:, first : first + 4]
            * (1.0 - tail[:, first : first + 4] * parity)
            / (dreal * dreal + dimag * dimag)
        )
        real_part = real_part + jnp.sum(factor * dreal, axis=-1)
        imag_part = imag_part - jnp.sum(factor * dimag, axis=-1)
    return (real_part, imag_part)


def convolve(gated, skip, filters, total, move_forward, move_back):
    pieces, block, width = gated.shape
    span = 2 * pieces
    outer_index = jnp.arange(span, dtype=jnp.int32)
    piece_index = jnp.arange(pieces, dtype=jnp.int32)
    outer_cos, outer_sin = angle_tables(outer_index, piece_index, span)
    real_part = jnp.einsum("kp,ptc->ktc", outer_cos, gated, precision=HIGHEST)
    imag_part = -jnp.einsum("kp,ptc->ktc", outer_sin, gated, precision=HIGHEST)
    times = jnp.arange(block, dtype=jnp.int32)
    twist_cos, twist_sin = angle_tables(outer_index, times, total)
    twist_cos = twist_cos[:, :, None]
    twist_sin = twist_sin[:, :, None]
    turned_real = twist_cos * real_part + twist_sin * imag_part
    turned_imag = twist_cos * imag_part - twist_sin * real_part
    moved = move_forward(jnp.stack([turned_real, turned_imag]))
    count = moved.shape[1]
    length = moved.shape[2]
    positions = jnp.arange(length, dtype=jnp.int32)
    inner_cos, inner_sin = angle_tables(positions, positions, length)
    freq_real = jnp.einsum("mt,ktc->kmc", inner_cos, moved[0], precision=HIGHEST) + jnp.einsum(
        "mt,ktc->kmc", inner_sin, moved[1], precision=HIGHEST
    )
    freq_imag = jnp.einsum("mt,ktc->kmc", inner_cos, moved[1], precision=HIGHEST) - jnp.einsum(
        "mt,ktc->kmc", inner_sin, moved[0], precision=HIGHEST
    )
    owned = jnp.arange(count, dtype=jnp.int32)
    freq = (owned[:, None] + span * positions[None, :]) % total
    filt_real, filt_imag = filter_spectrum(freq, total, *filters)
    prod_real = freq_real * filt_real - freq_imag * filt_imag
    prod_imag = freq_real * filt_imag + freq_imag * filt_real
    back_real = jnp.einsum("mt,kmc->ktc", inner_cos, prod_real, precision=HIGHEST) - jnp.einsum(
        "mt,kmc->ktc", inner_sin, prod_imag, precision=HIGHEST
    )
    back_imag = jnp.einsum("mt,kmc->ktc", inner_cos, prod_imag, precision=HIGHEST) + jnp.einsum(
        "mt,kmc->ktc", inner_sin, prod_real, precision=HIGHEST
    )
    undo_cos, undo_sin = angle_tables(owned, positions, total)
    undo_cos = undo_cos[:, :, None]
    undo_sin = undo_sin[:, :, None]
    untwist_real = undo_cos * back_real - undo_sin * back_imag
    untwist_imag = undo_cos * back_imag + undo_sin * back_real
    returned = move_back(jnp.stack([untwist_real, untwist_imag]))
    last_cos, last_sin = angle_tables(piece_index, outer_index, span)
    convolved = (
        jnp.einsum("pk,ktc->ptc", last_cos, returned[0], precision=HIGHEST)
        - jnp.einsum("pk,ktc->ptc", last_sin, returned[1], precision=HIGHEST)
    ) * (1.0 / total)
    return convolved + skip * gated


def unchanged(value):
    return value


def body(token_ids, vocab_table, short_filter, residue, decay, skip_gain):
    pieces = lax.axis_size("seq")
    place = lax.axis_index("seq")
    length = token_ids.shape[0]
    local = length // pieces
    share = vocab_table.shape[2]
    rim = short_filter.shape[0] - 1
    total = 2 * length
    rate = decay / length
    pole = jnp.exp(-rate)
    gap = -jnp.expm1(-rate)
    tail = jnp.exp(-decay)
    scale = residue * jnp.sqrt(2.0 * rate)
    first_channel = place * share
    chan_taps = lax.dynamic_slice_in_dim(short_filter, first_channel, share, 2)
    chan_filters = (
        lax.dynamic_slice_in_dim(pole, first_channel, share, 0),
        lax.dynamic_slice_in_dim(gap, first_channel, share, 0),
        lax.dynamic_slice_in_dim(tail, first_channel, share, 0),
        lax.dynamic_slice_in_dim(scale, first_channel, share, 0),
    )
    chan_skip = lax.dynamic_slice_in_dim(skip_gain, first_channel, share, 0)
    streams = jnp.take(vocab_table, token_ids, axis=0)
    padded = jnp.pad(streams, ((rim, 0), (0, 0), (0, 0)))
    mixed = short_conv(padded, chan_taps, length)
    query = mixed[:, 0]
    gated = (mixed[:, 1] * mixed[:, 2]).reshape(pieces, local, share)
    convolved = convolve(gated, chan_skip, chan_filters, total, unchanged, unchanged)
    output = (query * convolved.reshape(length, share)).astype(jnp.bfloat16)
    return lax.all_to_all(output, "seq", split_axis=0, concat_axis=1, tiled=True)


LANES = 128
SUB = 8
HALO = 8
UNROLL = 8
MESH = pl.DeviceIdType.MESH


def wide(row):
    return jnp.broadcast_to(row, (SUB, LANES))


def scan_kernel(
    pieces,
    local,
    width,
    modes,
    ids_ref,
    all_tab_ref,
    all_taps_ref,
    all_decay_ref,
    all_residue_ref,
    all_skip_ref,
    out_ref,
    tab_ref,
    taps_ref,
    decay_ref,
    residue_ref,
    skip_ref,
    load_sem,
    hot_ref,
    x_ref,
    query_ref,
    gated_ref,
    end_ref,
    begin_ref,
    coef_ref,
    turn_ref,
    send_ref,
    send_sem,
    recv_sem,
    own_sem,
):
    me = lax.axis_index("seq")
    half = pieces // 2
    near = me // half
    slots = pieces // SUB
    parts = half // SUB
    share = skip_ref.shape[1]
    vocab = tab_ref.shape[1]
    blocks = share // LANES
    length = pieces * local
    mine = pl.ds(pl.multiple_of(me * share, LANES), share)
    loads = (
        (all_tab_ref, tab_ref),
        (all_taps_ref.at[:, :, mine], taps_ref),
        (all_decay_ref.at[:, mine], decay_ref),
        (all_residue_ref.at[:, mine], residue_ref),
        (all_skip_ref.at[:, mine], skip_ref),
    )
    loads = [
        pltpu.make_async_copy(source, target, load_sem.at[i])
        for i, (source, target) in enumerate(loads)
    ]
    for load in loads:
        load.start()
    barrier = pltpu.get_barrier_semaphore()
    for step in range(1, pieces):
        peer = lax.rem(me + step, pieces)
        pl.semaphore_signal(barrier, inc=1, device_id={"seq": peer}, device_id_type=MESH)

    rows = (HALO + local) * pieces
    cut = rows // 4
    ids = ids_ref[...]
    before = jnp.where(
        lax.broadcasted_iota(jnp.int32, ids.shape, 0) == 0, -1, pltpu.roll(ids, 1, axis=0)
    )
    entry = lax.broadcasted_iota(jnp.int32, (pieces, vocab), 1)
    for t in range(-HALO, local):
        column = ids[:, t : t + 1] if t >= 0 else before[:, local + t : local + t + 1]
        hot_ref[(HALO + t) * pieces : (HALO + t + 1) * pieces, :] = jnp.where(
            column == entry, 1.0, 0.0
        ).astype(jnp.bfloat16)
    for load in loads:
        load.wait()

    def remote(block, peer, source):
        column = pl.ds(pl.multiple_of(source * share + block * LANES, LANES), LANES)
        return pltpu.make_async_remote_copy(
            src_ref=send_ref.at[block, peer],
            dst_ref=out_ref.at[:, column],
            send_sem=send_sem.at[block, peer],
            recv_sem=recv_sem.at[block, source],
            device_id={"seq": peer},
            device_id_type=MESH,
        )

    def own(block):
        column = pl.ds(pl.multiple_of(me * share + block * LANES, LANES), LANES)
        return pltpu.make_async_copy(send_ref.at[block, me], out_ref.at[:, column], own_sem.at[block])

    for block in range(blocks):
        lane = pl.ds(block * LANES, LANES)
        rate = decay_ref[:, lane] / length
        pole = jnp.exp(-rate)
        leap = jnp.exp(-rate * local)
        coef_ref[0] = pole
        coef_ref[1] = residue_ref[:, lane] * jnp.sqrt(2.0 * rate)
        skip = wide(skip_ref[:, lane])
        table = jnp.concatenate([tab_ref[j, :, lane] for j in range(3)], axis=1)
        for i in range(4):
            span = pl.ds(i * cut, cut)
            x_ref[span, :] = jnp.dot(hot_ref[span, :], table, preferred_element_type=jnp.float32)

        def first_pass(slot, _):
            base = pl.multiple_of(slot * SUB, SUB)
            poles = [wide(coef_ref[0, s : s + 1, :]) for s in range(modes)]
            taps = [
                [wide(taps_ref[j, lag : lag + 1, lane]) for lag in range(width)] for j in range(3)
            ]

            def step(i, state):
                state = list(state)
                mixed = []
                for j in range(3):
                    seen = {}
                    for t in range(1 - width, UNROLL):
                        at = pl.multiple_of((i * UNROLL + t + HALO) * pieces + base, SUB)
                        seen[t] = x_ref[pl.ds(at, SUB), j * LANES : (j + 1) * LANES]
                    totals = []
                    for t in range(UNROLL):
                        total = taps[j][0] * seen[t]
                        for lag in range(1, width):
                            total = total + taps[j][lag] * seen[t - lag]
                        totals.append(total)
                    mixed.append(totals)
                for t in range(UNROLL):
                    at = pl.multiple_of((i * UNROLL + t) * pieces + base, SUB)
                    gated = mixed[1][t] * mixed[2][t]
                    query_ref[pl.ds(at, SUB), :] = mixed[0][t]
                    gated_ref[pl.ds(at, SUB), :] = gated
                    for s in range(modes):
                        state[s] = poles[s] * state[s] + gated
                return tuple(state)

            zero = jnp.zeros((SUB, LANES), jnp.float32)
            state = lax.fori_loop(0, local // UNROLL, step, (zero,) * modes)
            for s in range(modes):
                end_ref[pl.ds(pl.multiple_of(s * pieces + base, SUB), SUB), :] = state[s]
            return 0

        lax.fori_loop(0, slots, first_pass, 0)
        carry = jnp.zeros((modes, LANES), jnp.float32)
        for k in range(pieces):
            begin_ref[pl.ds(k, modes, stride=pieces), :] = carry
            carry = leap * carry + end_ref[pl.ds(k, modes, stride=pieces), :]

        for side in range(2):
            group = near if side else 1 - near
            for part in range(parts):
                first = group * half + part * SUB
                base = pl.multiple_of(first, SUB)
                poles = [wide(coef_ref[0, s : s + 1, :]) for s in range(modes)]
                coefs = [wide(coef_ref[1, s : s + 1, :]) for s in range(modes)]

                def step(i, state):
                    state = list(state)
                    for t in range(UNROLL):
                        at = pl.multiple_of((i * UNROLL + t) * pieces + base, SUB)
                        gated = gated_ref[pl.ds(at, SUB), :]
                        terms = [skip * gated]
                        for s in range(modes):
                            state[s] = poles[s] * state[s] + gated
                            terms.append(coefs[s] * state[s])
                            if len(terms) == 5:
                                terms = [((terms[0] + terms[1]) + (terms[2] + terms[3])) + terms[4]]
                        total = terms[0]
                        for term in terms[1:]:
                            total = total + term
                        turn_ref[pl.ds(pl.multiple_of((i * UNROLL + t) * SUB, SUB), SUB), :] = (
                            query_ref[pl.ds(at, SUB), :] * total
                        )
                    return tuple(state)

                state = tuple(
                    begin_ref[pl.ds(pl.multiple_of(s * pieces + base, SUB), SUB), :]
                    for s in range(modes)
                )
                lax.fori_loop(0, local // UNROLL, step, state)
                for k in range(SUB):
                    send_ref[block, first + k] = turn_ref[pl.ds(k, local, stride=SUB), :].astype(
                        jnp.bfloat16
                    )
                if block == 0 and side == 0 and part == 0:
                    pl.semaphore_wait(barrier, pieces - 1)
                for k in range(SUB):
                    peer = first + lax.rem(me + k, SUB)
                    if side == 0:
                        remote(block, peer, me).start()
                    else:

                        @pl.when(peer != me)
                        def _():
                            remote(block, peer, me).start()

                        @pl.when(peer == me)
                        def _():
                            own(block).start()

    for block in range(blocks):
        own(block).wait()
        for step in range(1, pieces):
            remote(block, lax.rem(me + step, pieces), me).wait_send()
        for step in range(1, pieces):
            remote(block, me, lax.rem(me + step, pieces)).wait_recv()


def scan_body(token_ids, vocab_table, short_filter, residue, decay, skip_gain):
    pieces = lax.axis_size("seq")
    length = token_ids.shape[0]
    local = length // pieces
    vocab, streams, share = vocab_table.shape
    width = short_filter.shape[0]
    modes = decay.shape[1]
    blocks = share // LANES
    ids = token_ids.reshape(pieces, local)
    table = vocab_table.transpose(1, 0, 2)
    taps = short_filter.transpose(1, 0, 2)
    rows = (HALO + local) * pieces
    vmem = pl.BlockSpec(memory_space=pltpu.VMEM)
    return pl.pallas_call(
        functools.partial(scan_kernel, pieces, local, width, modes),
        out_shape=pltpu.VMEM((local, pieces * share), jnp.bfloat16),
        in_specs=[vmem] + [pl.BlockSpec(memory_space=pl.ANY)] * 5,
        out_specs=pl.BlockSpec(memory_space=pltpu.VMEM),
        scratch_shapes=[
            pltpu.VMEM((streams, vocab, share), vocab_table.dtype),
            pltpu.VMEM((streams, width, share), jnp.float32),
            pltpu.VMEM((modes, share), jnp.float32),
            pltpu.VMEM((modes, share), jnp.float32),
            pltpu.VMEM((1, share), jnp.float32),
            pltpu.SemaphoreType.DMA((5,)),
            pltpu.VMEM((rows, vocab), jnp.bfloat16),
            pltpu.VMEM((rows, streams * LANES), jnp.float32),
            pltpu.VMEM((length, LANES), jnp.float32),
            pltpu.VMEM((length, LANES), jnp.float32),
            pltpu.VMEM((modes * pieces, LANES), jnp.float32),
            pltpu.VMEM((modes * pieces, LANES), jnp.float32),
            pltpu.VMEM((2, modes, LANES), jnp.float32),
            pltpu.VMEM((local * SUB, LANES), jnp.float32),
            pltpu.VMEM((blocks, pieces, local, LANES), jnp.bfloat16),
            pltpu.SemaphoreType.DMA((blocks, pieces)),
            pltpu.SemaphoreType.DMA((blocks, pieces)),
            pltpu.SemaphoreType.DMA((blocks,)),
        ],
        compiler_params=pltpu.CompilerParams(collective_id=0, has_side_effects=True),
    )(ids, table, taps, decay.T, residue.T, skip_gain[None])


def fits(mesh, share, local, width):
    pieces = mesh.shape["seq"]
    return share % LANES == 0 and pieces % (2 * SUB) == 0 and local % 16 == 0 and width <= HALO + 1


def solution(mesh):
    placed = (P("groups"), P(None, None, "seq"), P(), P(), P(), P())

    def whole(token_ids, vocab_table, short_filter, residue, decay, skip_gain):
        pieces = mesh.shape["seq"]
        local = token_ids.shape[0] // (mesh.shape["groups"] * pieces)
        share = vocab_table.shape[2] // pieces
        chosen = scan_body if fits(mesh, share, local, short_filter.shape[0]) else body
        return jax.shard_map(
            chosen, mesh=mesh, in_specs=placed, out_specs=P(("groups", "seq"), None), check_vma=False
        )(token_ids, vocab_table, short_filter, residue, decay, skip_gain)

    return whole
```

```python
import functools
import math

import jax
import jax.numpy as jnp
from jax import lax
from jax.experimental import pallas as pl
from jax.experimental.pallas import tpu as pltpu
from jax.sharding import PartitionSpec as P

HIGHEST = lax.Precision.HIGHEST


def angle_tables(first_index, second_index, modulus):
    product = first_index[:, None] * second_index[None, :] % modulus
    angle = product.astype(jnp.float32) * (2.0 * math.pi / modulus)
    return (jnp.cos(angle), jnp.sin(angle))


def short_conv(padded, taps, count):
    width = taps.shape[0]
    total = jnp.zeros((count,) + padded.shape[1:], jnp.float32)
    for lag in range(width):
        start = width - 1 - lag
        total = total + taps[lag] * padded[start : start + count].astype(jnp.float32)
    return total


def filter_spectrum(freq, total, pole, gap, tail, scale):
    theta = freq.astype(jnp.float32) * (2.0 * math.pi / total)
    sine = jnp.sin(theta)[:, :, None, None]
    halfsq = (jnp.sin(0.5 * theta) ** 2)[:, :, None, None]
    parity = (1 - 2 * (freq % 2)).astype(jnp.float32)[:, :, None, None]
    shape_out = freq.shape + (pole.shape[0],)
    real_part = jnp.zeros(shape_out, jnp.float32)
    imag_part = jnp.zeros(shape_out, jnp.float32)
    for first in range(0, pole.shape[1], 4):
        part_pole = pole[:, first : first + 4]
        dreal = gap[:, first : first + 4] + 2.0 * part_pole * halfsq
        dimag = part_pole * sine
        factor = (
            scale[:, first : first + 4]
            * (1.0 - tail[:, first : first + 4] * parity)
            / (dreal * dreal + dimag * dimag)
        )
        real_part = real_part + jnp.sum(factor * dreal, axis=-1)
        imag_part = imag_part - jnp.sum(factor * dimag, axis=-1)
    return (real_part, imag_part)


def convolve(gated, skip, filters, total, move_forward, move_back):
    pieces, block, width = gated.shape
    span = 2 * pieces
    outer_index = jnp.arange(span, dtype=jnp.int32)
    piece_index = jnp.arange(pieces, dtype=jnp.int32)
    outer_cos, outer_sin = angle_tables(outer_index, piece_index, span)
    real_part = jnp.einsum("kp,ptc->ktc", outer_cos, gated, precision=HIGHEST)
    imag_part = -jnp.einsum("kp,ptc->ktc", outer_sin, gated, precision=HIGHEST)
    times = jnp.arange(block, dtype=jnp.int32)
    twist_cos, twist_sin = angle_tables(outer_index, times, total)
    twist_cos = twist_cos[:, :, None]
    twist_sin = twist_sin[:, :, None]
    turned_real = twist_cos * real_part + twist_sin * imag_part
    turned_imag = twist_cos * imag_part - twist_sin * real_part
    moved = move_forward(jnp.stack([turned_real, turned_imag]))
    count = moved.shape[1]
    length = moved.shape[2]
    positions = jnp.arange(length, dtype=jnp.int32)
    inner_cos, inner_sin = angle_tables(positions, positions, length)
    freq_real = jnp.einsum("mt,ktc->kmc", inner_cos, moved[0], precision=HIGHEST) + jnp.einsum(
        "mt,ktc->kmc", inner_sin, moved[1], precision=HIGHEST
    )
    freq_imag = jnp.einsum("mt,ktc->kmc", inner_cos, moved[1], precision=HIGHEST) - jnp.einsum(
        "mt,ktc->kmc", inner_sin, moved[0], precision=HIGHEST
    )
    owned = jnp.arange(count, dtype=jnp.int32)
    freq = (owned[:, None] + span * positions[None, :]) % total
    filt_real, filt_imag = filter_spectrum(freq, total, *filters)
    prod_real = freq_real * filt_real - freq_imag * filt_imag
    prod_imag = freq_real * filt_imag + freq_imag * filt_real
    back_real = jnp.einsum("mt,kmc->ktc", inner_cos, prod_real, precision=HIGHEST) - jnp.einsum(
        "mt,kmc->ktc", inner_sin, prod_imag, precision=HIGHEST
    )
    back_imag = jnp.einsum("mt,kmc->ktc", inner_cos, prod_imag, precision=HIGHEST) + jnp.einsum(
        "mt,kmc->ktc", inner_sin, prod_real, precision=HIGHEST
    )
    undo_cos, undo_sin = angle_tables(owned, positions, total)
    undo_cos = undo_cos[:, :, None]
    undo_sin = undo_sin[:, :, None]
    untwist_real = undo_cos * back_real - undo_sin * back_imag
    untwist_imag = undo_cos * back_imag + undo_sin * back_real
    returned = move_back(jnp.stack([untwist_real, untwist_imag]))
    last_cos, last_sin = angle_tables(piece_index, outer_index, span)
    convolved = (
        jnp.einsum("pk,ktc->ptc", last_cos, returned[0], precision=HIGHEST)
        - jnp.einsum("pk,ktc->ptc", last_sin, returned[1], precision=HIGHEST)
    ) * (1.0 / total)
    return convolved + skip * gated


def unchanged(value):
    return value


def body(token_ids, vocab_table, short_filter, residue, decay, skip_gain):
    pieces = lax.axis_size("seq")
    place = lax.axis_index("seq")
    length = token_ids.shape[0]
    local = length // pieces
    share = vocab_table.shape[2]
    rim = short_filter.shape[0] - 1
    total = 2 * length
    rate = decay / length
    pole = jnp.exp(-rate)
    gap = -jnp.expm1(-rate)
    tail = jnp.exp(-decay)
    scale = residue * jnp.sqrt(2.0 * rate)
    first_channel = place * share
    chan_taps = lax.dynamic_slice_in_dim(short_filter, first_channel, share, 2)
    chan_filters = (
        lax.dynamic_slice_in_dim(pole, first_channel, share, 0),
        lax.dynamic_slice_in_dim(gap, first_channel, share, 0),
        lax.dynamic_slice_in_dim(tail, first_channel, share, 0),
        lax.dynamic_slice_in_dim(scale, first_channel, share, 0),
    )
    chan_skip = lax.dynamic_slice_in_dim(skip_gain, first_channel, share, 0)
    streams = jnp.take(vocab_table, token_ids, axis=0)
    padded = jnp.pad(streams, ((rim, 0), (0, 0), (0, 0)))
    mixed = short_conv(padded, chan_taps, length)
    query = mixed[:, 0]
    gated = (mixed[:, 1] * mixed[:, 2]).reshape(pieces, local, share)
    convolved = convolve(gated, chan_skip, chan_filters, total, unchanged, unchanged)
    output = (query * convolved.reshape(length, share)).astype(jnp.bfloat16)
    return lax.all_to_all(output, "seq", split_axis=0, concat_axis=1, tiled=True)


LANES = 128
SUB = 8
HALO = 8
UNROLL = 8
CUTS = 4
SPLITS = 2
MESH = pl.DeviceIdType.MESH


def wide(row):
    return jnp.broadcast_to(row, (SUB, LANES))


def flip(value, mask, limit):
    result, bit = 0, 1
    while bit < limit:
        result = result + bit * ((value // bit + mask // bit) % 2)
        bit = 2 * bit
    return result


def scan_kernel(
    pieces,
    local,
    width,
    modes,
    ids_ref,
    all_tab_ref,
    all_taps_ref,
    all_decay_ref,
    all_residue_ref,
    all_skip_ref,
    out_ref,
    tab_ref,
    taps_ref,
    decay_ref,
    residue_ref,
    skip_ref,
    load_sem,
    hot_ref,
    x_ref,
    query_ref,
    gated_ref,
    end_ref,
    begin_ref,
    coef_ref,
    turn_ref,
    send_ref,
    send_sem,
    recv_sem,
    own_sem,
):
    me = lax.axis_index("seq")
    slots = pieces // SUB
    share = skip_ref.shape[1]
    vocab = tab_ref.shape[1]
    blocks = share // LANES
    length = pieces * local
    mine = pl.ds(pl.multiple_of(me * share, LANES), share)
    loads = (
        (all_tab_ref, tab_ref),
        (all_taps_ref.at[:, :, mine], taps_ref),
        (all_decay_ref.at[:, mine], decay_ref),
        (all_residue_ref.at[:, mine], residue_ref),
        (all_skip_ref.at[:, mine], skip_ref),
    )
    loads = [
        pltpu.make_async_copy(source, target, load_sem.at[i])
        for i, (source, target) in enumerate(loads)
    ]
    for load in loads:
        load.start()
    barrier = pltpu.get_barrier_semaphore()
    for step in range(1, pieces):
        peer = lax.rem(me + step, pieces)
        pl.semaphore_signal(barrier, inc=1, device_id={"seq": peer}, device_id_type=MESH)

    cut = (HALO + local) * pieces // CUTS
    ids = ids_ref[...]
    before = jnp.where(
        lax.broadcasted_iota(jnp.int32, ids.shape, 0) == 0, -1, pltpu.roll(ids, 1, axis=0)
    )
    entry = lax.broadcasted_iota(jnp.int32, (pieces, vocab), 1)
    count = (HALO + local) // CUTS

    def build(i):
        for t in range(i * count - HALO, (i + 1) * count - HALO):
            column = ids[:, t : t + 1] if t >= 0 else before[:, local + t : local + t + 1]
            hot_ref[(HALO + t) * pieces : (HALO + t + 1) * pieces, :] = jnp.where(
                column == entry, 1.0, 0.0
            ).astype(jnp.bfloat16)

    build(0)
    for load in loads:
        load.wait()

    height = local // SPLITS

    def place(block, part, source):
        return out_ref.at[
            pl.ds(part * height, height),
            pl.ds(pl.multiple_of(source * share + block * LANES, LANES), LANES),
        ]

    def remote(block, part, peer, source):
        return pltpu.make_async_remote_copy(
            src_ref=send_ref.at[block, peer, pl.ds(part * height, height)],
            dst_ref=place(block, part, source),
            send_sem=send_sem.at[block, part, peer],
            recv_sem=recv_sem.at[block, part, source],
            device_id={"seq": peer},
            device_id_type=MESH,
        )

    def own(block, part):
        return pltpu.make_async_copy(
            send_ref.at[block, me, pl.ds(part * height, height)],
            place(block, part, me),
            own_sem.at[block, part],
        )

    for block in range(blocks):
        lane = pl.ds(block * LANES, LANES)
        rate = decay_ref[:, lane] / length
        pole = jnp.exp(-rate)
        leap = jnp.exp(-rate * local)
        coef_ref[0] = pole
        coef_ref[1] = residue_ref[:, lane] * jnp.sqrt(2.0 * rate)
        skip = wide(skip_ref[:, lane])
        table = jnp.concatenate([tab_ref[j, :, lane] for j in range(3)], axis=1)
        for i in range(CUTS):
            if block == 0 and i + 1 < CUTS:
                build(i + 1)
            span = pl.ds(i * cut, cut)
            x_ref[span, :] = jnp.dot(hot_ref[span, :], table, preferred_element_type=jnp.float32)

        def first_pass(slot, _):
            base = pl.multiple_of(slot * SUB, SUB)
            poles = [wide(coef_ref[0, s : s + 1, :]) for s in range(modes)]
            taps = [
                [wide(taps_ref[j, lag : lag + 1, lane]) for lag in range(width)] for j in range(3)
            ]

            def step(i, state):
                state = list(state)
                mixed = []
                for j in range(3):
                    seen = {}
                    for t in range(1 - width, UNROLL):
                        at = pl.multiple_of((i * UNROLL + t + HALO) * pieces + base, SUB)
                        seen[t] = x_ref[pl.ds(at, SUB), j * LANES : (j + 1) * LANES]
                    totals = []
                    for t in range(UNROLL):
                        total = taps[j][0] * seen[t]
                        for lag in range(1, width):
                            total = total + taps[j][lag] * seen[t - lag]
                        totals.append(total)
                    mixed.append(totals)
                for t in range(UNROLL):
                    at = pl.multiple_of((i * UNROLL + t) * pieces + base, SUB)
                    gated = mixed[1][t] * mixed[2][t]
                    query_ref[pl.ds(at, SUB), :] = mixed[0][t]
                    gated_ref[pl.ds(at, SUB), :] = gated
                    for s in range(modes):
                        state[s] = poles[s] * state[s] + gated
                return tuple(state)

            zero = jnp.zeros((SUB, LANES), jnp.float32)
            state = lax.fori_loop(0, local // UNROLL, step, (zero,) * modes)
            for s in range(modes):
                end_ref[pl.ds(pl.multiple_of(s * pieces + base, SUB), SUB), :] = state[s]
            return 0

        lax.fori_loop(0, slots, first_pass, 0)
        carry = jnp.zeros((modes, LANES), jnp.float32)
        for k in range(pieces):
            begin_ref[pl.ds(k, modes, stride=pieces), :] = carry
            carry = leap * carry + end_ref[pl.ds(k, modes, stride=pieces), :]

        for far in range(slots - 1, -1, -1):
            first = flip(me // SUB, far, slots) * SUB
            base = pl.multiple_of(first, SUB)
            poles = [wide(coef_ref[0, s : s + 1, :]) for s in range(modes)]
            coefs = [wide(coef_ref[1, s : s + 1, :]) for s in range(modes)]

            def step(i, state):
                state = list(state)
                for t in range(UNROLL):
                    at = pl.multiple_of((i * UNROLL + t) * pieces + base, SUB)
                    gated = gated_ref[pl.ds(at, SUB), :]
                    terms = [skip * gated]
                    for s in range(modes):
                        state[s] = poles[s] * state[s] + gated
                        terms.append(coefs[s] * state[s])
                        if len(terms) == 5:
                            terms = [((terms[0] + terms[1]) + (terms[2] + terms[3])) + terms[4]]
                    total = terms[0]
                    for term in terms[1:]:
                        total = total + term
                    turn_ref[pl.ds(pl.multiple_of((i * UNROLL + t) * SUB, SUB), SUB), :] = (
                        query_ref[pl.ds(at, SUB), :] * total
                    )
                return tuple(state)

            state = tuple(
                begin_ref[pl.ds(pl.multiple_of(s * pieces + base, SUB), SUB), :]
                for s in range(modes)
            )
            for part in range(SPLITS):
                low = part * height
                state = lax.fori_loop(low // UNROLL, (low + height) // UNROLL, step, state)
                for k in range(SUB):
                    send_ref[block, first + k, low : low + height, :] = turn_ref[
                        pl.ds(low * SUB + k, height, stride=SUB), :
                    ].astype(jnp.bfloat16)
                if block == 0 and far == slots - 1 and part == 0:
                    pl.semaphore_wait(barrier, pieces - 1)
                for k in range(SUB):
                    if far == 0 and k == 0:
                        own(block, part).start()
                    else:
                        remote(block, part, flip(me, far * SUB + k, pieces), me).start()

    for block in range(blocks):
        for part in range(SPLITS):
            own(block, part).wait()
            for step in range(1, pieces):
                remote(block, part, flip(me, step, pieces), me).wait_send()
            for step in range(1, pieces):
                remote(block, part, me, flip(me, step, pieces)).wait_recv()


def scan_body(token_ids, vocab_table, short_filter, residue, decay, skip_gain):
    pieces = lax.axis_size("seq")
    length = token_ids.shape[0]
    local = length // pieces
    vocab, streams, share = vocab_table.shape
    width = short_filter.shape[0]
    modes = decay.shape[1]
    blocks = share // LANES
    ids = token_ids.reshape(pieces, local)
    table = vocab_table.transpose(1, 0, 2)
    taps = short_filter.transpose(1, 0, 2)
    rows = (HALO + local) * pieces
    vmem = pl.BlockSpec(memory_space=pltpu.VMEM)
    return pl.pallas_call(
        functools.partial(scan_kernel, pieces, local, width, modes),
        out_shape=pltpu.VMEM((local, pieces * share), jnp.bfloat16),
        in_specs=[vmem] + [pl.BlockSpec(memory_space=pl.ANY)] * 5,
        out_specs=pl.BlockSpec(memory_space=pltpu.VMEM),
        scratch_shapes=[
            pltpu.VMEM((streams, vocab, share), vocab_table.dtype),
            pltpu.VMEM((streams, width, share), jnp.float32),
            pltpu.VMEM((modes, share), jnp.float32),
            pltpu.VMEM((modes, share), jnp.float32),
            pltpu.VMEM((1, share), jnp.float32),
            pltpu.SemaphoreType.DMA((5,)),
            pltpu.VMEM((rows, vocab), jnp.bfloat16),
            pltpu.VMEM((rows, streams * LANES), jnp.float32),
            pltpu.VMEM((length, LANES), jnp.float32),
            pltpu.VMEM((length, LANES), jnp.float32),
            pltpu.VMEM((modes * pieces, LANES), jnp.float32),
            pltpu.VMEM((modes * pieces, LANES), jnp.float32),
            pltpu.VMEM((2, modes, LANES), jnp.float32),
            pltpu.VMEM((local * SUB, LANES), jnp.float32),
            pltpu.VMEM((blocks, pieces, local, LANES), jnp.bfloat16),
            pltpu.SemaphoreType.DMA((blocks, SPLITS, pieces)),
            pltpu.SemaphoreType.DMA((blocks, SPLITS, pieces)),
            pltpu.SemaphoreType.DMA((blocks, SPLITS)),
        ],
        compiler_params=pltpu.CompilerParams(collective_id=0, has_side_effects=True),
    )(ids, table, taps, decay.T, residue.T, skip_gain[None])


def fits(mesh, share, local, width):
    pieces = mesh.shape["seq"]
    even = pieces % (2 * SUB) == 0 and pieces & (pieces - 1) == 0
    return share % LANES == 0 and even and local % (16 * SPLITS) == 0 and width <= HALO + 1


def solution(mesh):
    placed = (P("groups"), P(None, None, "seq"), P(), P(), P(), P())

    def whole(token_ids, vocab_table, short_filter, residue, decay, skip_gain):
        pieces = mesh.shape["seq"]
        local = token_ids.shape[0] // (mesh.shape["groups"] * pieces)
        share = vocab_table.shape[2] // pieces
        chosen = scan_body if fits(mesh, share, local, short_filter.shape[0]) else body
        return jax.shard_map(
            chosen, mesh=mesh, in_specs=placed, out_specs=P(("groups", "seq"), None), check_vma=False
        )(token_ids, vocab_table, short_filter, residue, decay, skip_gain)

    return whole
```

```python
import functools
import math

import jax
import jax.numpy as jnp
from jax import lax
from jax.experimental import pallas as pl
from jax.experimental.pallas import tpu as pltpu
from jax.sharding import PartitionSpec as P

HIGHEST = lax.Precision.HIGHEST


def angle_tables(first_index, second_index, modulus):
    product = first_index[:, None] * second_index[None, :] % modulus
    angle = product.astype(jnp.float32) * (2.0 * math.pi / modulus)
    return (jnp.cos(angle), jnp.sin(angle))


def short_conv(padded, taps, count):
    width = taps.shape[0]
    total = jnp.zeros((count,) + padded.shape[1:], jnp.float32)
    for lag in range(width):
        start = width - 1 - lag
        total = total + taps[lag] * padded[start : start + count].astype(jnp.float32)
    return total


def filter_spectrum(freq, total, pole, gap, tail, scale):
    theta = freq.astype(jnp.float32) * (2.0 * math.pi / total)
    sine = jnp.sin(theta)[:, :, None, None]
    halfsq = (jnp.sin(0.5 * theta) ** 2)[:, :, None, None]
    parity = (1 - 2 * (freq % 2)).astype(jnp.float32)[:, :, None, None]
    shape_out = freq.shape + (pole.shape[0],)
    real_part = jnp.zeros(shape_out, jnp.float32)
    imag_part = jnp.zeros(shape_out, jnp.float32)
    for first in range(0, pole.shape[1], 4):
        part_pole = pole[:, first : first + 4]
        dreal = gap[:, first : first + 4] + 2.0 * part_pole * halfsq
        dimag = part_pole * sine
        factor = (
            scale[:, first : first + 4]
            * (1.0 - tail[:, first : first + 4] * parity)
            / (dreal * dreal + dimag * dimag)
        )
        real_part = real_part + jnp.sum(factor * dreal, axis=-1)
        imag_part = imag_part - jnp.sum(factor * dimag, axis=-1)
    return (real_part, imag_part)


def convolve(gated, skip, filters, total, move_forward, move_back):
    pieces, block, width = gated.shape
    span = 2 * pieces
    outer_index = jnp.arange(span, dtype=jnp.int32)
    piece_index = jnp.arange(pieces, dtype=jnp.int32)
    outer_cos, outer_sin = angle_tables(outer_index, piece_index, span)
    real_part = jnp.einsum("kp,ptc->ktc", outer_cos, gated, precision=HIGHEST)
    imag_part = -jnp.einsum("kp,ptc->ktc", outer_sin, gated, precision=HIGHEST)
    times = jnp.arange(block, dtype=jnp.int32)
    twist_cos, twist_sin = angle_tables(outer_index, times, total)
    twist_cos = twist_cos[:, :, None]
    twist_sin = twist_sin[:, :, None]
    turned_real = twist_cos * real_part + twist_sin * imag_part
    turned_imag = twist_cos * imag_part - twist_sin * real_part
    moved = move_forward(jnp.stack([turned_real, turned_imag]))
    count = moved.shape[1]
    length = moved.shape[2]
    positions = jnp.arange(length, dtype=jnp.int32)
    inner_cos, inner_sin = angle_tables(positions, positions, length)
    freq_real = jnp.einsum("mt,ktc->kmc", inner_cos, moved[0], precision=HIGHEST) + jnp.einsum(
        "mt,ktc->kmc", inner_sin, moved[1], precision=HIGHEST
    )
    freq_imag = jnp.einsum("mt,ktc->kmc", inner_cos, moved[1], precision=HIGHEST) - jnp.einsum(
        "mt,ktc->kmc", inner_sin, moved[0], precision=HIGHEST
    )
    owned = jnp.arange(count, dtype=jnp.int32)
    freq = (owned[:, None] + span * positions[None, :]) % total
    filt_real, filt_imag = filter_spectrum(freq, total, *filters)
    prod_real = freq_real * filt_real - freq_imag * filt_imag
    prod_imag = freq_real * filt_imag + freq_imag * filt_real
    back_real = jnp.einsum("mt,kmc->ktc", inner_cos, prod_real, precision=HIGHEST) - jnp.einsum(
        "mt,kmc->ktc", inner_sin, prod_imag, precision=HIGHEST
    )
    back_imag = jnp.einsum("mt,kmc->ktc", inner_cos, prod_imag, precision=HIGHEST) + jnp.einsum(
        "mt,kmc->ktc", inner_sin, prod_real, precision=HIGHEST
    )
    undo_cos, undo_sin = angle_tables(owned, positions, total)
    undo_cos = undo_cos[:, :, None]
    undo_sin = undo_sin[:, :, None]
    untwist_real = undo_cos * back_real - undo_sin * back_imag
    untwist_imag = undo_cos * back_imag + undo_sin * back_real
    returned = move_back(jnp.stack([untwist_real, untwist_imag]))
    last_cos, last_sin = angle_tables(piece_index, outer_index, span)
    convolved = (
        jnp.einsum("pk,ktc->ptc", last_cos, returned[0], precision=HIGHEST)
        - jnp.einsum("pk,ktc->ptc", last_sin, returned[1], precision=HIGHEST)
    ) * (1.0 / total)
    return convolved + skip * gated


def unchanged(value):
    return value


def body(token_ids, vocab_table, short_filter, residue, decay, skip_gain):
    pieces = lax.axis_size("seq")
    place = lax.axis_index("seq")
    length = token_ids.shape[0]
    local = length // pieces
    share = vocab_table.shape[2]
    rim = short_filter.shape[0] - 1
    total = 2 * length
    rate = decay / length
    pole = jnp.exp(-rate)
    gap = -jnp.expm1(-rate)
    tail = jnp.exp(-decay)
    scale = residue * jnp.sqrt(2.0 * rate)
    first_channel = place * share
    chan_taps = lax.dynamic_slice_in_dim(short_filter, first_channel, share, 2)
    chan_filters = (
        lax.dynamic_slice_in_dim(pole, first_channel, share, 0),
        lax.dynamic_slice_in_dim(gap, first_channel, share, 0),
        lax.dynamic_slice_in_dim(tail, first_channel, share, 0),
        lax.dynamic_slice_in_dim(scale, first_channel, share, 0),
    )
    chan_skip = lax.dynamic_slice_in_dim(skip_gain, first_channel, share, 0)
    streams = jnp.take(vocab_table, token_ids, axis=0)
    padded = jnp.pad(streams, ((rim, 0), (0, 0), (0, 0)))
    mixed = short_conv(padded, chan_taps, length)
    query = mixed[:, 0]
    gated = (mixed[:, 1] * mixed[:, 2]).reshape(pieces, local, share)
    convolved = convolve(gated, chan_skip, chan_filters, total, unchanged, unchanged)
    output = (query * convolved.reshape(length, share)).astype(jnp.bfloat16)
    return lax.all_to_all(output, "seq", split_axis=0, concat_axis=1, tiled=True)


LANES = 128
SUB = 8
HALO = 8
UNROLL = 8
CUTS = 4
SPLITS = 1
MESH = pl.DeviceIdType.MESH


def wide(row):
    return jnp.broadcast_to(row, (SUB, LANES))


def toggles(value, limit):
    steps, bit = [], 1
    while bit < limit:
        steps.append((bit, bit - 2 * bit * (value // bit % 2)))
        bit = 2 * bit
    return steps


def flip(value, steps, mask):
    for bit, step in steps:
        if mask & bit:
            value = value + step
    return value


def scan_kernel(
    pieces,
    local,
    width,
    modes,
    ids_ref,
    all_tab_ref,
    all_taps_ref,
    all_decay_ref,
    all_residue_ref,
    all_skip_ref,
    out_ref,
    tab_ref,
    taps_ref,
    decay_ref,
    residue_ref,
    skip_ref,
    load_sem,
    hot_ref,
    x_ref,
    query_ref,
    gated_ref,
    end_ref,
    begin_ref,
    coef_ref,
    turn_ref,
    send_ref,
    send_sem,
    recv_sem,
    own_sem,
):
    me = lax.axis_index("seq")
    slots = pieces // SUB
    steps = toggles(me, pieces)
    share = skip_ref.shape[1]
    vocab = tab_ref.shape[1]
    blocks = share // LANES
    length = pieces * local
    mine = pl.ds(pl.multiple_of(me * share, LANES), share)
    loads = (
        (all_tab_ref, tab_ref),
        (all_taps_ref.at[:, :, mine], taps_ref),
        (all_decay_ref.at[:, mine], decay_ref),
        (all_residue_ref.at[:, mine], residue_ref),
        (all_skip_ref.at[:, mine], skip_ref),
    )
    loads = [
        pltpu.make_async_copy(source, target, load_sem.at[i])
        for i, (source, target) in enumerate(loads)
    ]
    for load in loads:
        load.start()
    barrier = pltpu.get_barrier_semaphore()
    for mask in range(1, pieces):
        peer = flip(me, steps, mask)
        pl.semaphore_signal(barrier, inc=1, device_id={"seq": peer}, device_id_type=MESH)

    cut = (HALO + local) * pieces // CUTS
    ids = ids_ref[...]
    before = jnp.where(
        lax.broadcasted_iota(jnp.int32, ids.shape, 0) == 0, -1, pltpu.roll(ids, 1, axis=0)
    )
    entry = lax.broadcasted_iota(jnp.int32, (pieces, vocab), 1)
    count = (HALO + local) // CUTS

    def build(i):
        for t in range(i * count - HALO, (i + 1) * count - HALO):
            column = ids[:, t : t + 1] if t >= 0 else before[:, local + t : local + t + 1]
            hot_ref[(HALO + t) * pieces : (HALO + t + 1) * pieces, :] = jnp.where(
                column == entry, 1.0, 0.0
            ).astype(jnp.bfloat16)

    build(0)
    for load in loads:
        load.wait()

    height = local // SPLITS

    def place(block, part, source):
        return out_ref.at[
            pl.ds(part * height, height),
            pl.ds(pl.multiple_of(source * share + block * LANES, LANES), LANES),
        ]

    def remote(block, part, mask, peer, source):
        return pltpu.make_async_remote_copy(
            src_ref=send_ref.at[block, peer, pl.ds(part * height, height)],
            dst_ref=place(block, part, source),
            send_sem=send_sem.at[block, part, mask],
            recv_sem=recv_sem.at[block, part, mask],
            device_id={"seq": peer},
            device_id_type=MESH,
        )

    def own(block, part):
        return pltpu.make_async_copy(
            send_ref.at[block, me, pl.ds(part * height, height)],
            place(block, part, me),
            own_sem.at[block, part],
        )

    for block in range(blocks):
        lane = pl.ds(block * LANES, LANES)
        rate = decay_ref[:, lane] / length
        pole = jnp.exp(-rate)
        leap = jnp.exp(-rate * local)
        coef_ref[0] = pole
        coef_ref[1] = residue_ref[:, lane] * jnp.sqrt(2.0 * rate)
        skip = wide(skip_ref[:, lane])
        table = jnp.concatenate([tab_ref[j, :, lane] for j in range(3)], axis=1)
        for i in range(CUTS):
            if block == 0 and i + 1 < CUTS:
                build(i + 1)
            span = pl.ds(i * cut, cut)
            x_ref[span, :] = jnp.dot(hot_ref[span, :], table, preferred_element_type=jnp.float32)

        def first_pass(slot, _):
            base = pl.multiple_of(slot * SUB, SUB)
            poles = [wide(coef_ref[0, s : s + 1, :]) for s in range(modes)]
            taps = [
                [wide(taps_ref[j, lag : lag + 1, lane]) for lag in range(width)] for j in range(3)
            ]

            def step(i, state):
                state = list(state)
                mixed = []
                for j in range(3):
                    seen = {}
                    for t in range(1 - width, UNROLL):
                        at = pl.multiple_of((i * UNROLL + t + HALO) * pieces + base, SUB)
                        seen[t] = x_ref[pl.ds(at, SUB), j * LANES : (j + 1) * LANES]
                    totals = []
                    for t in range(UNROLL):
                        total = taps[j][0] * seen[t]
                        for lag in range(1, width):
                            total = total + taps[j][lag] * seen[t - lag]
                        totals.append(total)
                    mixed.append(totals)
                for t in range(UNROLL):
                    at = pl.multiple_of((i * UNROLL + t) * pieces + base, SUB)
                    gated = mixed[1][t] * mixed[2][t]
                    query_ref[pl.ds(at, SUB), :] = mixed[0][t]
                    gated_ref[pl.ds(at, SUB), :] = gated
                    for s in range(modes):
                        state[s] = poles[s] * state[s] + gated
                return tuple(state)

            zero = jnp.zeros((SUB, LANES), jnp.float32)
            state = lax.fori_loop(0, local // UNROLL, step, (zero,) * modes)
            for s in range(modes):
                end_ref[pl.ds(pl.multiple_of(s * pieces + base, SUB), SUB), :] = state[s]
            return 0

        lax.fori_loop(0, slots, first_pass, 0)
        carry = jnp.zeros((modes, LANES), jnp.float32)
        for k in range(pieces):
            begin_ref[pl.ds(k, modes, stride=pieces), :] = carry
            carry = leap * carry + end_ref[pl.ds(k, modes, stride=pieces), :]

        for far in range(slots - 1, -1, -1):
            first = flip(me // SUB * SUB, steps, far * SUB)
            base = pl.multiple_of(first, SUB)
            poles = [wide(coef_ref[0, s : s + 1, :]) for s in range(modes)]
            coefs = [wide(coef_ref[1, s : s + 1, :]) for s in range(modes)]

            def step(i, state):
                state = list(state)
                for t in range(UNROLL):
                    at = pl.multiple_of((i * UNROLL + t) * pieces + base, SUB)
                    gated = gated_ref[pl.ds(at, SUB), :]
                    terms = [skip * gated]
                    for s in range(modes):
                        state[s] = poles[s] * state[s] + gated
                        terms.append(coefs[s] * state[s])
                        if len(terms) == 5:
                            terms = [((terms[0] + terms[1]) + (terms[2] + terms[3])) + terms[4]]
                    total = terms[0]
                    for term in terms[1:]:
                        total = total + term
                    turn_ref[pl.ds(pl.multiple_of((i * UNROLL + t) * SUB, SUB), SUB), :] = (
                        query_ref[pl.ds(at, SUB), :] * total
                    )
                return tuple(state)

            state = tuple(
                begin_ref[pl.ds(pl.multiple_of(s * pieces + base, SUB), SUB), :]
                for s in range(modes)
            )
            for part in range(SPLITS):
                low = part * height
                state = lax.fori_loop(low // UNROLL, (low + height) // UNROLL, step, state)
                for k in range(SUB):
                    send_ref[block, first + k, low : low + height, :] = turn_ref[
                        pl.ds(low * SUB + k, height, stride=SUB), :
                    ].astype(jnp.bfloat16)
                if block == 0 and far == slots - 1 and part == 0:
                    pl.semaphore_wait(barrier, pieces - 1)
                for k in range(SUB):
                    if far == 0 and k == 0:
                        own(block, part).start()
                    else:
                        mask = far * SUB + k
                        remote(block, part, mask, flip(me, steps, mask), me).start()

    for block in range(blocks):
        for part in range(SPLITS):
            own(block, part).wait()
            for mask in range(1, pieces):
                peer = flip(me, steps, mask)
                remote(block, part, mask, peer, me).wait_send()
                remote(block, part, mask, me, peer).wait_recv()


def scan_body(token_ids, vocab_table, short_filter, residue, decay, skip_gain):
    pieces = lax.axis_size("seq")
    length = token_ids.shape[0]
    local = length // pieces
    vocab, streams, share = vocab_table.shape
    width = short_filter.shape[0]
    modes = decay.shape[1]
    blocks = share // LANES
    ids = token_ids.reshape(pieces, local)
    table = vocab_table.transpose(1, 0, 2)
    taps = short_filter.transpose(1, 0, 2)
    rows = (HALO + local) * pieces
    vmem = pl.BlockSpec(memory_space=pltpu.VMEM)
    return pl.pallas_call(
        functools.partial(scan_kernel, pieces, local, width, modes),
        out_shape=pltpu.VMEM((local, pieces * share), jnp.bfloat16),
        in_specs=[vmem] + [pl.BlockSpec(memory_space=pl.ANY)] * 5,
        out_specs=pl.BlockSpec(memory_space=pltpu.VMEM),
        scratch_shapes=[
            pltpu.VMEM((streams, vocab, share), vocab_table.dtype),
            pltpu.VMEM((streams, width, share), jnp.float32),
            pltpu.VMEM((modes, share), jnp.float32),
            pltpu.VMEM((modes, share), jnp.float32),
            pltpu.VMEM((1, share), jnp.float32),
            pltpu.SemaphoreType.DMA((5,)),
            pltpu.VMEM((rows, vocab), jnp.bfloat16),
            pltpu.VMEM((rows, streams * LANES), jnp.float32),
            pltpu.VMEM((length, LANES), jnp.float32),
            pltpu.VMEM((length, LANES), jnp.float32),
            pltpu.VMEM((modes * pieces, LANES), jnp.float32),
            pltpu.VMEM((modes * pieces, LANES), jnp.float32),
            pltpu.VMEM((2, modes, LANES), jnp.float32),
            pltpu.VMEM((local * SUB, LANES), jnp.float32),
            pltpu.VMEM((blocks, pieces, local, LANES), jnp.bfloat16),
            pltpu.SemaphoreType.DMA((blocks, SPLITS, pieces)),
            pltpu.SemaphoreType.DMA((blocks, SPLITS, pieces)),
            pltpu.SemaphoreType.DMA((blocks, SPLITS)),
        ],
        compiler_params=pltpu.CompilerParams(collective_id=0, has_side_effects=True),
    )(ids, table, taps, decay.T, residue.T, skip_gain[None])


def fits(mesh, share, local, width):
    pieces = mesh.shape["seq"]
    even = pieces % (2 * SUB) == 0 and pieces & (pieces - 1) == 0
    return share % LANES == 0 and even and local % (16 * SPLITS) == 0 and width <= HALO + 1


def solution(mesh):
    placed = (P("groups"), P(None, None, "seq"), P(), P(), P(), P())

    def whole(token_ids, vocab_table, short_filter, residue, decay, skip_gain):
        pieces = mesh.shape["seq"]
        local = token_ids.shape[0] // (mesh.shape["groups"] * pieces)
        share = vocab_table.shape[2] // pieces
        chosen = scan_body if fits(mesh, share, local, short_filter.shape[0]) else body
        return jax.shard_map(
            chosen, mesh=mesh, in_specs=placed, out_specs=P(("groups", "seq"), None), check_vma=False
        )(token_ids, vocab_table, short_filter, residue, decay, skip_gain)

    return whole
```
